32 devices in a mesh: rows: 8 (over z, x), width: 4 (over y, core).
Axes of the slice: x: 2, y: 2, z: 4, core: 2. Of those that a mesh axis runs over, the one named last changes fastest.
Arguments:
- queries: bfloat16 [6144, 4096], P('rows', 'width')
- passages: bfloat16 [2048, 4096], P('rows', 'width')
- neighbor_ids: int32 [24, 4], P('rows'), may hold values from 0 to 7, as said below
- counts: int32 [24], P('rows'), may hold values from 1 to 4
Outputs:
- losses: float32 [6144], P(('rows', 'width'))
- grad_queries: bfloat16 [6144, 4096], P('rows', 'width')
- grad_passages: bfloat16 [2048, 4096], P('rows', 'width')
The draws below stay inside these ranges and needn't reach their ends.
Inputs may be any that keep to these rules, and one draw needn't show every extreme that they name: `neighbor_ids`: entry k of row c, for k below counts[c], names a passage block one or two blocks away from block c // 3 in the cyclic order of 8 blocks, all different within the row; the remaining entries name block c // 3.
All inputs are finite; a program needn't handle non-finite values.
Results may differ from the reference program's by a relative error of at most 0.0049.
Values may be sent and summed in bfloat16 or wider, within the bound.
A program may use at most 64 MiB of HBM per device.

```python
import math
import jax
import jax.numpy as jnp
from jax import lax

D = 4096
BLOCK = 256
SLOTS = 4
QBLK_DEV = 3
PBLOCKS = 8
QBLOCKS = 24
QUERY_TOTAL = 6144
PASSAGES = 2048


def passage_table(key):
    base = jax.random.fold_in(key, 101)
    first_key, second_key = jax.random.split(base, 2)
    values = jax.random.normal(first_key, (PASSAGES, D), jnp.float32)
    scales = jnp.exp(jax.random.uniform(second_key, (PASSAGES, 1), jnp.float32, math.log(0.5), math.log(2.0)))
    return values * scales * D ** (-0.5)


def draw_passages(key, part):
    return passage_table(key).astype(jnp.bfloat16)


def draw_queries(key, part):
    table = passage_table(key)
    base = jax.random.fold_in(key, 202)
    first_key, second_key = jax.random.split(base, 2)
    per_dev = QBLK_DEV * BLOCK
    rows_index = jnp.arange(QUERY_TOTAL, dtype=jnp.int32)
    positive_rows = rows_index // per_dev * BLOCK + rows_index % per_dev % BLOCK
    positive = table[positive_rows]
    noise = jax.random.normal(first_key, (QUERY_TOTAL, D), jnp.float32)
    scales = jnp.exp(jax.random.uniform(second_key, (QUERY_TOTAL, 1), jnp.float32, math.log(0.5), math.log(4.0)))
    values = scales * (noise * D ** (-0.5) + 0.08 * positive)
    return values.astype(jnp.bfloat16)


def dispatch_mapping(key):
    base = jax.random.fold_in(key, 303)
    first_key, second_key = jax.random.split(base, 2)
    tally_numbers = jax.random.randint(first_key, (QBLOCKS,), 1, SLOTS + 1, jnp.int32)
    tally_numbers = tally_numbers.at[0].set(1).at[QBLOCKS - 1].set(1).at[QBLOCKS // 2].set(SLOTS)
    row_keys = jax.random.split(second_key, QBLOCKS)
    order = jax.vmap(lambda single: jax.random.permutation(single, SLOTS))(row_keys).astype(jnp.int32)
    offsets = jnp.array([-2, -1, 1, 2], jnp.int32)[order]
    owner = jnp.arange(QBLOCKS, dtype=jnp.int32) // QBLK_DEV
    block_ids = (owner[:, None] + offsets + PBLOCKS) % PBLOCKS
    used = jnp.arange(SLOTS, dtype=jnp.int32)[None, :] < tally_numbers[:, None]
    block_ids = jnp.where(used, block_ids, owner[:, None])
    return (block_ids.astype(jnp.int32), tally_numbers.astype(jnp.int32))


def draw_neighbor_ids(key, part):
    return dispatch_mapping(key)[0]


def draw_counts(key, part):
    return dispatch_mapping(key)[1]


def setup_inputs(seed: int = 0) -> dict:
    seeds = jax.random.split(jax.random.key(seed), 5)
    return {
        "queries": draw_queries(jax.random.fold_in(seeds[4], 71), 0),
        "passages": draw_passages(jax.random.fold_in(seeds[4], 71), 0),
        "neighbor_ids": draw_neighbor_ids(jax.random.fold_in(seeds[4], 71), 0),
        "counts": draw_counts(jax.random.fold_in(seeds[4], 71), 0),
    }


inverse_sharpness_scale = 50.0


def block_mask(neighbor_rows, count_rows, owner, nblocks):
    listed = jnp.arange(neighbor_rows.shape[1], dtype=jnp.int32)[None, :] < count_rows[:, None]
    columns = []
    for offset in range(5):
        if offset == 2:
            columns.append(jnp.ones((neighbor_rows.shape[0],), dtype=bool))
        else:
            target = (owner + offset - 2 + nblocks) % nblocks
            columns.append(jnp.any(listed & (neighbor_rows == target), axis=1))
    return jnp.stack(columns, axis=1)


def score_grads(pairwise_logits, row_exists_flag, local_rows):
    width_block = pairwise_logits.shape[1] // 5
    column_mask = jnp.repeat(row_exists_flag, width_block, axis=1)
    masked = jnp.where(column_mask, pairwise_logits, -jnp.inf)
    row_max = jnp.max(masked, axis=1, keepdims=True)
    expon = jnp.exp(masked - row_max)
    row_sum = jnp.sum(expon, axis=1, keepdims=True)
    normalized_probability = expon / row_sum
    positive_col = 2 * width_block + local_rows % width_block
    matching_pair_mask = jnp.arange(pairwise_logits.shape[1], dtype=jnp.int32)[None, :] == positive_col[:, None]
    positive = jnp.sum(jnp.where(matching_pair_mask, pairwise_logits, 0.0), axis=1)
    losses = row_max[:, 0] + jnp.log(row_sum[:, 0]) - positive
    derivative_entries = (inverse_sharpness_scale * (normalized_probability - matching_pair_mask.astype(jnp.float32))).astype(jnp.bfloat16)
    return losses, derivative_entries


def reference(queries, passages, neighbor_ids, counts):
    nblocks = PASSAGES // BLOCK
    per_dev = QBLK_DEV * BLOCK

    def owner_step(total, owner):
        query_rows = lax.dynamic_slice_in_dim(queries, (owner * per_dev).astype(jnp.int32), per_dev, 0)
        blocks = [(owner + offset - 2 + nblocks) % nblocks for offset in range(5)]
        candidates = jnp.concatenate(
            [lax.dynamic_slice_in_dim(passages, (blk * BLOCK).astype(jnp.int32), BLOCK, 0) for blk in blocks], axis=0)
        neighbor_rows = lax.dynamic_slice_in_dim(neighbor_ids, (owner * QBLK_DEV).astype(jnp.int32), QBLK_DEV, 0)
        count_rows = lax.dynamic_slice_in_dim(counts, (owner * QBLK_DEV).astype(jnp.int32), QBLK_DEV, 0)
        present = block_mask(neighbor_rows, count_rows, owner, nblocks)
        row_exists_flag = jnp.repeat(present, BLOCK, axis=0)
        pairwise_logits = inverse_sharpness_scale * lax.dot_general(
            query_rows, candidates, (((1,), (1,)), ((), ())), preferred_element_type=jnp.float32)
        losses, derivative_entries = score_grads(pairwise_logits, row_exists_flag, jnp.arange(per_dev, dtype=jnp.int32))
        grad_q = jnp.dot(derivative_entries, candidates, preferred_element_type=jnp.float32).astype(jnp.bfloat16)
        passage_terms = lax.dot_general(
            derivative_entries, query_rows, (((0,), (0,)), ((), ())), preferred_element_type=jnp.float32)
        for offset in range(5):
            start = (blocks[offset] * BLOCK).astype(jnp.int32)
            current = lax.dynamic_slice_in_dim(total, start, BLOCK, 0)
            term = passage_terms[offset * BLOCK:(offset + 1) * BLOCK]
            if offset != 2:
                term = term.astype(jnp.bfloat16).astype(jnp.float32)
            total = lax.dynamic_update_slice_in_dim(total, current + term, start, 0)
        return total, (losses, grad_q)

    start_total = jnp.zeros((PASSAGES, D), jnp.float32)
    total, (losses, grad_q) = lax.scan(owner_step, start_total, jnp.arange(nblocks, dtype=jnp.int32))
    return losses.reshape(QUERY_TOTAL), grad_q.reshape(QUERY_TOTAL, D), total.astype(jnp.bfloat16)
```

```python
import functools

import jax
import jax.numpy as jnp
from jax import lax
from jax.experimental import pallas as pl
from jax.experimental.pallas import tpu as pltpu
from jax.sharding import PartitionSpec as P

MESH = pl.DeviceIdType.MESH
SCALE = 50.0
PIECES = 2
OWN, AHEAD, BEHIND, PAIR, RELAY = 0, 1, 2, 3, 4
SLOTS = 5
RETURN_ORDER = (RELAY, BEHIND, AHEAD, PAIR, OWN)

NT = (((1,), (1,)), ((), ()))
TN = (((0,), (0,)), ((), ()))
NN = (((1,), (0,)), ((), ()))


def dot(a, b, dims):
    return lax.dot_general(a, b, dims, preferred_element_type=jnp.float32)


def copies_needed():
    gather = 4 * PIECES
    scores = SLOTS * 3
    grads = SLOTS * 3
    terms = 4 * PIECES
    return gather + scores + grads + terms


def kernel(
    nrows, ids_ref, counts_ref, q_ref, p_ref, loss_ref, gq_ref, gp_ref,
    pbuf, spart, rs1, rs2s, rs2r, gbuf, lossbuf, term_own, term_ahead,
    tsend, trecv, send_sem, recv_sem,
):
    r = lax.axis_index("rows")
    w = lax.axis_index("width")
    par = lax.rem(r, 2)
    step = 2 - 4 * par
    pair = r + 1 - 2 * par
    ahead = lax.rem(r + step + nrows, nrows)
    behind = lax.rem(r - step + nrows, nrows)
    core = lax.rem(w, 2)
    side = w + 1 - 2 * core
    across = lax.rem(w + 2, 4)
    diagonal = lax.rem(side + 2, 4)
    block, width = p_ref.shape
    share = q_ref.shape[0] // 4

    to_pair, to_ahead, to_behind = {"rows": pair}, {"rows": ahead}, {"rows": behind}
    to_side, to_across = {"width": side}, {"width": across}

    barrier = pltpu.get_barrier_semaphore()
    for device in (to_pair, to_ahead, to_behind, to_side, to_across):
        pl.semaphore_signal(barrier, inc=1, device_id=device, device_id_type=MESH)
    pl.semaphore_wait(barrier, 5)

    started = []

    def send(src, dst, device):
        n = len(started)
        copy = pltpu.make_async_remote_copy(
            src_ref=src, dst_ref=dst, send_sem=send_sem.at[n], recv_sem=recv_sem.at[n],
            device_id=device, device_id_type=MESH,
        )
        copy.start()
        started.append(copy)
        return copy

    rows_piece = block // PIECES
    piece = [pl.ds(k * rows_piece, rows_piece) for k in range(PIECES)]
    arrive = {AHEAD: [], BEHIND: [], PAIR: [], RELAY: []}
    for k in range(PIECES):
        arrive[AHEAD].append(send(p_ref.at[piece[k]], pbuf.at[AHEAD - 1, piece[k]], to_behind))
        arrive[PAIR].append(send(p_ref.at[piece[k]], pbuf.at[PAIR - 1, piece[k]], to_pair))
        arrive[BEHIND].append(send(p_ref.at[piece[k]], pbuf.at[BEHIND - 1, piece[k]], to_ahead))

    def candidates(slot):
        return p_ref if slot == OWN else pbuf.at[slot - 1]

    first, second = {}, {}

    def score_block(slot):
        part = dot(q_ref[...], candidates(slot)[...], NT)
        spart[slot] = part.reshape(4, share, block)
        far = send(spart.at[slot, diagonal], rs1.at[slot, 1], to_side)
        near = send(spart.at[slot, side], rs1.at[slot, 0], to_side)
        first[slot] = (far, near)

    def score_pass_on(slot):
        first[slot][0].wait_recv()
        rs2s[slot] = spart[slot, across] + rs1[slot, 1]
        second[slot] = send(rs2s.at[slot], rs2r.at[slot], to_across)

    score_block(OWN)
    score_pass_on(OWN)
    for k in range(PIECES):
        arrive[PAIR][k].wait_recv()
    score_block(PAIR)
    for k in range(PIECES):
        arrive[AHEAD][k].wait_recv()
        arrive[RELAY].append(
            send(pbuf.at[AHEAD - 1, piece[k]], pbuf.at[RELAY - 1, piece[k]], to_pair))
    score_pass_on(PAIR)
    score_block(AHEAD)
    score_pass_on(AHEAD)
    for k in range(PIECES):
        arrive[BEHIND][k].wait_recv()
    score_block(BEHIND)
    score_pass_on(BEHIND)
    for k in range(PIECES):
        arrive[RELAY][k].wait_recv()
    score_block(RELAY)
    score_pass_on(RELAY)

    offsets = (0, step, -step, pair - r, r - pair)
    targets = [lax.rem(r + offset + nrows, nrows) for offset in offsets]
    nblk = ids_ref.shape[0]
    present = []
    for slot in range(1, SLOTS):
        flags = []
        for c in range(nblk):
            flag = jnp.int32(0)
            for k in range(ids_ref.shape[1]):
                hit = jnp.logical_and(k < counts_ref[c], ids_ref[c, k] == targets[slot])
                flag = jnp.maximum(flag, jnp.where(hit, jnp.int32(1), jnp.int32(0)))
            flags.append(flag)
        present.append(flags)

    for slot in range(SLOTS):
        first[slot][1].wait_recv()
        second[slot].wait_recv()

    tile = 32

    @pl.loop(0, share // tile)
    def _(i):
        at = pl.ds(pl.multiple_of(i * tile, tile), tile)
        row = w * share + i * tile + lax.broadcasted_iota(jnp.int32, (tile, block), 0)
        col = lax.broadcasted_iota(jnp.int32, (tile, block), 1)
        is_pos = col == lax.rem(row, block)
        which = row // block
        logits = []
        for slot in range(SLOTS):
            s = (spart[slot, w, at] + rs1[slot, 0, at] + rs2r[slot, at]) * SCALE
            if slot != OWN:
                flags = present[slot - 1]
                on = jnp.full((tile, block), flags[0], jnp.int32)
                for c in range(1, nblk):
                    on = jnp.where(which == c, flags[c], on)
                s = jnp.where(on > 0, s, -jnp.inf)
            logits.append(s)
        top = functools.reduce(jnp.maximum, logits)
        top = jnp.max(top, axis=1, keepdims=True)
        expon = [jnp.exp(s - top) for s in logits]
        total = jnp.sum(functools.reduce(jnp.add, expon), axis=1, keepdims=True)
        positive = jnp.sum(jnp.where(is_pos, logits[OWN], 0.0), axis=1, keepdims=True)
        loss = top + jnp.log(total) - positive
        lossbuf[at] = jnp.broadcast_to(loss, (tile, lossbuf.shape[1]))
        for slot in range(SLOTS):
            weight = expon[slot] / total
            if slot == OWN:
                weight = weight - jnp.where(is_pos, 1.0, 0.0)
            gbuf[slot, w, at] = (SCALE * weight).astype(jnp.bfloat16)

    from_across, from_side, from_diagonal = {}, {}, {}
    for slot in RETURN_ORDER:
        from_across[slot] = send(gbuf.at[slot, w], gbuf.at[slot, w], to_across)
        from_side[slot] = send(gbuf.at[slot, w], gbuf.at[slot, w], to_side)

    n = lossbuf.shape[1]
    eye = (lax.broadcasted_iota(jnp.int32, (share, n), 0)
           == lax.broadcasted_iota(jnp.int32, (share, n), 1))
    loss_ref[...] = jnp.sum(jnp.where(eye, lossbuf[...], 0.0), axis=0, keepdims=True)[:, :share]

    cols = width // PIECES
    merged = {}
    for slot in RETURN_ORDER:
        from_across[slot].wait_recv()
        from_diagonal[slot] = send(gbuf.at[slot, across], gbuf.at[slot, across], to_side)
        from_side[slot].wait_recv()
        from_diagonal[slot].wait_recv()
        grads = gbuf[slot].reshape(4 * share, block)
        for k in range(PIECES):
            term = dot(grads, q_ref[:, k * cols:(k + 1) * cols], TN)
            if slot == OWN:
                term_own[k] = term
            elif slot == AHEAD:
                term_ahead[k] = term
            else:
                tsend[slot - 1, k] = term.astype(jnp.bfloat16)
                device = to_behind if slot == BEHIND else to_pair
                merged[slot, k] = send(tsend.at[slot - 1, k], trecv.at[slot - 1, k], device)
    for k in range(PIECES):
        merged[RELAY, k].wait_recv()
        both = term_ahead[k] + trecv[RELAY - 1, k].astype(jnp.float32)
        tsend[AHEAD - 1, k] = both.astype(jnp.bfloat16)
        merged[AHEAD, k] = send(tsend.at[AHEAD - 1, k], trecv.at[AHEAD - 1, k], to_ahead)

    tile_cols = 256

    @pl.loop(0, width // tile_cols)
    def _(j):
        at = pl.ds(pl.multiple_of(j * tile_cols, tile_cols), tile_cols)
        total = dot(gbuf[OWN].reshape(4 * share, block), p_ref[:, at], NN)
        for slot in range(1, SLOTS):
            total += dot(gbuf[slot].reshape(4 * share, block), pbuf[slot - 1, :, at], NN)
        gq_ref[:, at] = total.astype(jnp.bfloat16)

    for k in range(PIECES):
        total = term_own[k]
        for slot in (PAIR, BEHIND, AHEAD):
            merged[slot, k].wait_recv()
            total += trecv[slot - 1, k].astype(jnp.float32)
        gp_ref[:, k * cols:(k + 1) * cols] = total.astype(jnp.bfloat16)

    for copy in started:
        copy.wait_send()


def per_device(queries, passages, neighbor_ids, counts):
    nrows = lax.axis_size("rows")
    assert lax.axis_size("width") == 4 and nrows % 2 == 0
    per_dev, width = queries.shape
    block = passages.shape[0]
    share = per_dev // 4
    lanes = -(-share // 128) * 128
    vmem = pl.BlockSpec(memory_space=pltpu.VMEM)
    smem = pl.BlockSpec(memory_space=pltpu.SMEM)
    bf16, f32 = jnp.bfloat16, jnp.float32
    ncopies = copies_needed()
    losses, grad_q, grad_p = pl.pallas_call(
        functools.partial(kernel, nrows),
        out_shape=(
            jax.ShapeDtypeStruct((1, share), f32),
            jax.ShapeDtypeStruct((per_dev, width), bf16),
            jax.ShapeDtypeStruct((block, width), bf16),
        ),
        in_specs=[smem, smem, vmem, vmem],
        out_specs=(vmem, vmem, vmem),
        scratch_shapes=[
            pltpu.VMEM((SLOTS - 1, block, width), bf16),
            pltpu.VMEM((SLOTS, 4, share, block), f32),
            pltpu.VMEM((SLOTS, 2, share, block), f32),
            pltpu.VMEM((SLOTS, share, block), f32),
            pltpu.VMEM((SLOTS, share, block), f32),
            pltpu.VMEM((SLOTS, 4, share, block), bf16),
            pltpu.VMEM((share, lanes), f32),
            pltpu.VMEM((PIECES, block, width // PIECES), f32),
            pltpu.VMEM((PIECES, block, width // PIECES), f32),
            pltpu.VMEM((SLOTS - 1, PIECES, block, width // PIECES), bf16),
            pltpu.VMEM((SLOTS - 1, PIECES, block, width // PIECES), bf16),
            pltpu.SemaphoreType.DMA((ncopies,)),
            pltpu.SemaphoreType.DMA((ncopies,)),
        ],
        compiler_params=pltpu.CompilerParams(
            collective_id=0, has_side_effects=True, vmem_limit_bytes=50 * 1024 * 1024
        ),
    )(neighbor_ids, counts, queries, passages)
    return losses.reshape(share), grad_q, grad_p


def solution(mesh):
    return jax.shard_map(
        per_device,
        mesh=mesh,
        in_specs=(P("rows", "width"), P("rows", "width"), P("rows", None), P("rows")),
        out_specs=(P(("rows", "width")), P("rows", "width"), P("rows", "width")),
        check_vma=False,
    )
```

```python
import functools

import jax
import jax.numpy as jnp
from jax import lax
from jax.experimental import pallas as pl
from jax.experimental.pallas import tpu as pltpu
from jax.sharding import PartitionSpec as P

MESH = pl.DeviceIdType.MESH
SCALE = 50.0
PIECES = 2
OWN, AHEAD, BEHIND, PAIR, RELAY = 0, 1, 2, 3, 4
SLOTS = 5
RETURN_ORDER = (
    (RELAY, 0), (BEHIND, 0), (RELAY, 1), (BEHIND, 1), (AHEAD, 0), (PAIR, 0), (AHEAD, 1), (PAIR, 1),
    (OWN, 0), (OWN, 1),
)

NT = (((1,), (1,)), ((), ()))
TN = (((0,), (0,)), ((), ()))
NN = (((1,), (0,)), ((), ()))


def dot(a, b, dims):
    return lax.dot_general(a, b, dims, preferred_element_type=jnp.float32)


def copies_needed():
    gather = 4 * PIECES
    scores = SLOTS * PIECES * 3
    grads = SLOTS * PIECES * 3
    terms = 4 * PIECES
    return gather + scores + grads + terms


def kernel(
    nrows, lists_hbm, q_hbm, p_hbm, loss_ref, gq_ref, gp_ref,
    pbuf, spart, rs1, rs2s, rs2r, gbuf, lossbuf, term_own, term_ahead,
    tsend, trecv, lists_ref, q_ref, p_ref, local_sem, send_sem, recv_sem,
):
    r = lax.axis_index("rows")
    w = lax.axis_index("width")
    par = lax.rem(r, 2)
    step = 2 - 4 * par
    pair = r + 1 - 2 * par
    ahead = lax.rem(r + step + nrows, nrows)
    behind = lax.rem(r - step + nrows, nrows)
    core = lax.rem(w, 2)
    side = w + 1 - 2 * core
    across = lax.rem(w + 2, 4)
    diagonal = lax.rem(side + 2, 4)
    block, width = p_ref.shape
    share = q_ref.shape[0] // 4

    to_pair, to_ahead, to_behind = {"rows": pair}, {"rows": ahead}, {"rows": behind}
    to_side, to_across = {"width": side}, {"width": across}

    local = [
        pltpu.make_async_copy(src, dst, local_sem.at[n])
        for n, (src, dst) in enumerate((
            (p_hbm, p_ref), (q_hbm, q_ref), (lists_hbm, lists_ref)))
    ]
    for copy in local:
        copy.start()

    barrier = pltpu.get_barrier_semaphore()
    for device in (to_pair, to_ahead, to_behind, to_side, to_across):
        pl.semaphore_signal(barrier, inc=1, device_id=device, device_id_type=MESH)
    pl.semaphore_wait(barrier, 5)

    started = []

    def send(src, dst, device):
        n = len(started)
        copy = pltpu.make_async_remote_copy(
            src_ref=src, dst_ref=dst, send_sem=send_sem.at[n], recv_sem=recv_sem.at[n],
            device_id=device, device_id_type=MESH,
        )
        copy.start()
        started.append(copy)
        return copy

    unit = block // PIECES
    piece = [pl.ds(k * unit, unit) for k in range(PIECES)]
    arrive = {}

    def pass_block(slot, k, src, device):
        arrive[slot, k] = send(src.at[piece[k]], pbuf.at[slot - 1, piece[k]], device)

    for k in range(PIECES):
        pass_block(AHEAD, k, p_hbm, to_behind)
        pass_block(PAIR, k, p_hbm, to_pair)
    sent = []

    def behind(k):
        arrive[AHEAD, k].wait_send()
        sent.append(id(arrive[AHEAD, k]))
        pass_block(BEHIND, k, p_hbm, to_ahead)

    def relay(k):
        arrive[AHEAD, k].wait_recv()
        pass_block(RELAY, k, pbuf.at[AHEAD - 1], to_pair)

    first, second, pending = {}, {}, []

    def pass_on():
        slot, k = pending.pop(0)
        first[slot, k][0].wait_recv()
        rs2s[slot, k] = spart[slot, k, across] + rs1[slot, k, 1]
        second[slot, k] = send(rs2s.at[slot, k], rs2r.at[slot, k], to_across)

    def score(slot, k):
        if slot in (PAIR, BEHIND, RELAY):
            arrive[slot, k].wait_recv()
        rows = p_ref[piece[k]] if slot == OWN else pbuf[slot - 1, piece[k]]
        spart[slot, k] = dot(q_ref[...], rows, NT).reshape(4, share, unit)
        first[slot, k] = (
            send(spart.at[slot, k, diagonal], rs1.at[slot, k, 1], to_side),
            send(spart.at[slot, k, side], rs1.at[slot, k, 0], to_side),
        )
        pending.append((slot, k))
        if len(pending) > 1:
            pass_on()

    for copy in local:
        copy.wait()
    for k in range(PIECES):
        score(OWN, k)
    for k in range(PIECES):
        behind(k)
        relay(k)
        score(PAIR, k)
        score(AHEAD, k)
    for k in range(PIECES):
        score(BEHIND, k)
        score(RELAY, k)
    pass_on()

    offsets = (0, step, -step, pair - r, r - pair)
    targets = [lax.rem(r + offset + nrows, nrows) for offset in offsets]
    nblk, nslots = lists_ref.shape[0], lists_ref.shape[1] - 1
    present = []
    for slot in range(1, SLOTS):
        flags = []
        for c in range(nblk):
            flag = jnp.int32(0)
            for k in range(nslots):
                hit = jnp.logical_and(k < lists_ref[c, nslots], lists_ref[c, k] == targets[slot])
                flag = jnp.maximum(flag, jnp.where(hit, jnp.int32(1), jnp.int32(0)))
            flags.append(flag)
        present.append(flags)

    for key in first:
        first[key][1].wait_recv()
        second[key].wait_recv()

    tile = 32
    keys = [(slot, k) for slot in range(SLOTS) for k in range(PIECES)]

    @pl.loop(0, share // tile)
    def _(i):
        at = pl.ds(pl.multiple_of(i * tile, tile), tile)
        row = w * share + i * tile + lax.broadcasted_iota(jnp.int32, (tile, unit), 0)
        col = lax.broadcasted_iota(jnp.int32, (tile, unit), 1)
        pos = lax.rem(row, block)
        which = row // block
        masks = []
        for flags in present:
            on = jnp.full((tile, unit), flags[0], jnp.int32)
            for c in range(1, nblk):
                on = jnp.where(which == c, flags[c], on)
            masks.append(on > 0)
        logits, positives = [], []
        for slot, k in keys:
            s = (spart[slot, k, w, at] + rs1[slot, k, 0, at] + rs2r[slot, k, at]) * SCALE
            if slot == OWN:
                positives.append(jnp.where(col + k * unit == pos, s, 0.0))
            else:
                s = jnp.where(masks[slot - 1], s, -jnp.inf)
            logits.append(s)
        top = jnp.max(functools.reduce(jnp.maximum, logits), axis=1, keepdims=True)
        expon = [jnp.exp(s - top) for s in logits]
        total = jnp.sum(functools.reduce(jnp.add, expon), axis=1, keepdims=True)
        positive = jnp.sum(functools.reduce(jnp.add, positives), axis=1, keepdims=True)
        loss = top + jnp.log(total) - positive
        lossbuf[at] = jnp.broadcast_to(loss, (tile, lossbuf.shape[1]))
        factor = SCALE / total
        for (slot, k), e in zip(keys, expon):
            g = e * factor
            if slot == OWN:
                g = g - jnp.where(col + k * unit == pos, SCALE, 0.0)
            gbuf[slot, k, w, at] = g.astype(jnp.bfloat16)

    from_across, from_side, from_diagonal = {}, {}, {}
    for slot, k in RETURN_ORDER:
        mine = gbuf.at[slot, k, w]
        from_across[slot, k] = send(mine, mine, to_across)
        from_side[slot, k] = send(mine, mine, to_side)

    n = lossbuf.shape[1]
    eye = (lax.broadcasted_iota(jnp.int32, (share, n), 0)
           == lax.broadcasted_iota(jnp.int32, (share, n), 1))
    loss_ref[...] = jnp.sum(jnp.where(eye, lossbuf[...], 0.0), axis=0, keepdims=True)[:, :share]

    merged = {}
    tiles = 2
    cols = width // tiles

    def relay_grads(slot, k):
        from_across[slot, k].wait_recv()
        other = gbuf.at[slot, k, across]
        from_diagonal[slot, k] = send(other, other, to_side)

    def term_piece(slot, k):
        from_side[slot, k].wait_recv()
        from_diagonal[slot, k].wait_recv()
        grads = gbuf[slot, k].reshape(4 * share, unit)
        for j in range(tiles):
            at = slice(j * cols, (j + 1) * cols)
            term = dot(grads, q_ref[:, at], TN)
            if slot == OWN:
                term_own[piece[k], at] = term
            elif slot == AHEAD:
                term_ahead[piece[k], at] = term
            else:
                tsend[slot - 1, piece[k], at] = term.astype(jnp.bfloat16)
        if slot not in (OWN, AHEAD):
            device = to_behind if slot == BEHIND else to_pair
            merged[slot, k] = send(
                tsend.at[slot - 1, piece[k]], trecv.at[slot - 1, piece[k]], device)

    relay_grads(*RETURN_ORDER[0])
    for here, later in zip(RETURN_ORDER, RETURN_ORDER[1:] + (None,)):
        term_piece(*here)
        if later is not None:
            relay_grads(*later)
    for k in range(PIECES):
        merged[RELAY, k].wait_recv()
        both = term_ahead[piece[k]] + trecv[RELAY - 1, piece[k]].astype(jnp.float32)
        tsend[AHEAD - 1, piece[k]] = both.astype(jnp.bfloat16)
        merged[AHEAD, k] = send(
            tsend.at[AHEAD - 1, piece[k]], trecv.at[AHEAD - 1, piece[k]], to_ahead)

    tile_cols = 256

    @pl.loop(0, width // tile_cols)
    def _(j):
        at = pl.ds(pl.multiple_of(j * tile_cols, tile_cols), tile_cols)
        total = None
        for slot in range(SLOTS):
            for k in range(PIECES):
                rows = p_ref[piece[k], at] if slot == OWN else pbuf[slot - 1, piece[k], at]
                part = dot(gbuf[slot, k].reshape(4 * share, unit), rows, NN)
                total = part if total is None else total + part
        gq_ref[:, at] = total.astype(jnp.bfloat16)

    for k in range(PIECES):
        total = term_own[piece[k]]
        for slot in (PAIR, BEHIND, AHEAD):
            merged[slot, k].wait_recv()
            total += trecv[slot - 1, piece[k]].astype(jnp.float32)
        gp_ref[piece[k]] = total.astype(jnp.bfloat16)

    for copy in started:
        if id(copy) not in sent:
            copy.wait_send()


def store_kernel(*refs):
    *pairs, sems = refs
    half = len(pairs) // 2
    copies = [
        pltpu.make_async_copy(src, dst, sems.at[n])
        for n, (src, dst) in enumerate(zip(pairs[:half], pairs[half:]))
    ]
    for copy in copies:
        copy.start()
    for copy in copies:
        copy.wait()


def store(*arrays):
    return pl.pallas_call(
        store_kernel,
        out_shape=tuple(jax.ShapeDtypeStruct(a.shape, a.dtype) for a in arrays),
        in_specs=[pl.BlockSpec(memory_space=pl.ANY)] * len(arrays),
        out_specs=tuple(pl.BlockSpec(memory_space=pltpu.HBM) for a in arrays),
        scratch_shapes=[pltpu.SemaphoreType.DMA((len(arrays),))],
        compiler_params=pltpu.CompilerParams(vmem_limit_bytes=2 * 1024 * 1024),
    )(*arrays)


def per_device(queries, passages, neighbor_ids, counts):
    nrows = lax.axis_size("rows")
    assert lax.axis_size("width") == 4 and nrows % 2 == 0
    per_dev, width = queries.shape
    block = passages.shape[0]
    share = per_dev // 4
    unit = block // PIECES
    lanes = -(-share // 128) * 128
    vmem = pl.BlockSpec(memory_space=pltpu.VMEM)
    hbm = pl.BlockSpec(memory_space=pltpu.HBM)
    bf16, f32 = jnp.bfloat16, jnp.float32
    ncopies = copies_needed()
    lists = jnp.concatenate([neighbor_ids, counts[:, None]], axis=1)
    results = pl.pallas_call(
        functools.partial(kernel, nrows),
        out_shape=(
            jax.ShapeDtypeStruct((1, share), f32),
            jax.ShapeDtypeStruct((per_dev, width), bf16),
            jax.ShapeDtypeStruct((block, width), bf16),
        ),
        in_specs=[hbm, hbm, hbm],
        out_specs=(vmem, vmem, vmem),
        scratch_shapes=[
            pltpu.VMEM((SLOTS - 1, block, width), bf16),
            pltpu.VMEM((SLOTS, PIECES, 4, share, unit), f32),
            pltpu.VMEM((SLOTS, PIECES, 2, share, unit), f32),
            pltpu.VMEM((SLOTS, PIECES, share, unit), f32),
            pltpu.VMEM((SLOTS, PIECES, share, unit), f32),
            pltpu.VMEM((SLOTS, PIECES, 4, share, unit), bf16),
            pltpu.VMEM((share, lanes), f32),
            pltpu.VMEM((block, width), f32),
            pltpu.VMEM((block, width), f32),
            pltpu.VMEM((SLOTS - 1, block, width), bf16),
            pltpu.VMEM((SLOTS - 1, block, width), bf16),
            pltpu.SMEM(lists.shape, jnp.int32),
            pltpu.VMEM((per_dev, width), bf16),
            pltpu.VMEM((block, width), bf16),
            pltpu.SemaphoreType.DMA((3,)),
            pltpu.SemaphoreType.DMA((ncopies,)),
            pltpu.SemaphoreType.DMA((ncopies,)),
        ],
        compiler_params=pltpu.CompilerParams(
            collective_id=0, has_side_effects=True, vmem_limit_bytes=50 * 1024 * 1024
        ),
    )(lists, queries, passages)
    losses, grad_q, grad_p = store(*results)
    return losses.reshape(share), grad_q, grad_p


def solution(mesh):
    return jax.shard_map(
        per_device,
        mesh=mesh,
        in_specs=(P("rows", "width"), P("rows", "width"), P("rows", None), P("rows")),
        out_specs=(P(("rows", "width")), P("rows", "width"), P("rows", "width")),
        check_vma=False,
    )
```

```python
import functools

import jax
import jax.numpy as jnp
from jax import lax
from jax.experimental import pallas as pl
from jax.experimental.pallas import tpu as pltpu
from jax.sharding import PartitionSpec as P

MESH = pl.DeviceIdType.MESH
SCALE = 50.0
PIECES = 2
OWN, AHEAD, BEHIND, PAIR, RELAY = 0, 1, 2, 3, 4
SLOTS = 5
RETURN_ORDER = (
    (RELAY, 0), (BEHIND, 0), (RELAY, 1), (BEHIND, 1), (AHEAD, 0), (PAIR, 0), (AHEAD, 1), (PAIR, 1),
    (OWN, 0), (OWN, 1),
)

NT = (((1,), (1,)), ((), ()))
TN = (((0,), (0,)), ((), ()))
NN = (((1,), (0,)), ((), ()))


def dot(a, b, dims):
    return lax.dot_general(a, b, dims, preferred_element_type=jnp.float32)


def copies_needed():
    gather = 6 * PIECES
    scores = SLOTS * PIECES * 3
    grads = SLOTS * PIECES * 3
    terms = 4 * PIECES
    return gather + scores + grads + terms


def kernel(
    nrows, lists_hbm, q_hbm, p_hbm, loss_ref, gq_ref, gp_ref,
    pbuf, spart, rs1, rs2s, rs2r, gbuf, lossbuf, term_own, term_ahead,
    tsend, trecv, lists_ref, q_ref, p_ref, local_sem, send_sem, recv_sem,
):
    r = lax.axis_index("rows")
    w = lax.axis_index("width")
    par = lax.rem(r, 2)
    step = 2 - 4 * par
    pair = r + 1 - 2 * par
    ahead = lax.rem(r + step + nrows, nrows)
    behind = lax.rem(r - step + nrows, nrows)
    core = lax.rem(w, 2)
    side = w + 1 - 2 * core
    across = lax.rem(w + 2, 4)
    diagonal = lax.rem(side + 2, 4)
    block, width = p_ref.shape
    share = q_ref.shape[0] // 4

    to_pair, to_ahead, to_behind = {"rows": pair}, {"rows": ahead}, {"rows": behind}
    to_side, to_across = {"width": side}, {"width": across}

    local = [
        pltpu.make_async_copy(src, dst, local_sem.at[n])
        for n, (src, dst) in enumerate((
            (p_hbm, p_ref), (q_hbm, q_ref), (lists_hbm, lists_ref)))
    ]
    for copy in local:
        copy.start()

    barrier = pltpu.get_barrier_semaphore()
    for device in (to_pair, to_ahead, to_behind, to_side, to_across):
        pl.semaphore_signal(barrier, inc=1, device_id=device, device_id_type=MESH)
    pl.semaphore_wait(barrier, 5)

    started = []

    def send(src, dst, device):
        n = len(started)
        copy = pltpu.make_async_remote_copy(
            src_ref=src, dst_ref=dst, send_sem=send_sem.at[n], recv_sem=recv_sem.at[n],
            device_id=device, device_id_type=MESH,
        )
        copy.start()
        started.append(copy)
        return copy

    unit = block // PIECES
    piece = [pl.ds(k * unit, unit) for k in range(PIECES)]
    arrive = {}

    small = unit // 2
    strip = [pl.ds(m * small, small) for m in range(2 * PIECES)]

    def pass_block(slot, k, src, device):
        arrive[slot, k] = send(src.at[piece[k]], pbuf.at[slot - 1, piece[k]], device)

    def pass_strips(slot, k, src, device):
        for m in (2 * k, 2 * k + 1):
            arrive[slot, m] = send(src.at[strip[m]], pbuf.at[slot - 1, strip[m]], device)

    for k in range(PIECES):
        pass_block(AHEAD, k, p_hbm, to_behind)
        pass_block(PAIR, k, p_hbm, to_pair)
    sent = []

    def behind(k):
        arrive[AHEAD, k].wait_send()
        sent.append(id(arrive[AHEAD, k]))
        pass_strips(BEHIND, k, p_hbm, to_ahead)

    def relay(k):
        arrive[AHEAD, k].wait_recv()
        pass_strips(RELAY, k, pbuf.at[AHEAD - 1], to_pair)

    first, second, pending = {}, {}, []

    def pass_on():
        slot, k = pending.pop(0)
        first[slot, k][0].wait_recv()
        rs2s[slot, k] = spart[slot, k, across] + rs1[slot, k, 1]
        second[slot, k] = send(rs2s.at[slot, k], rs2r.at[slot, k], to_across)

    def score(slot, k):
        if slot in (BEHIND, RELAY):
            m = 2 * k + (slot == RELAY)
            arrive[BEHIND, m].wait_recv()
            arrive[RELAY, m].wait_recv()
            rows = jnp.concatenate(
                [pbuf[BEHIND - 1, strip[m]], pbuf[RELAY - 1, strip[m]]], axis=0)
        elif slot == OWN:
            rows = p_ref[piece[k]]
        else:
            if slot == PAIR:
                arrive[PAIR, k].wait_recv()
            rows = pbuf[slot - 1, piece[k]]
        spart[slot, k] = dot(q_ref[...], rows, NT).reshape(4, share, unit)
        first[slot, k] = (
            send(spart.at[slot, k, diagonal], rs1.at[slot, k, 1], to_side),
            send(spart.at[slot, k, side], rs1.at[slot, k, 0], to_side),
        )
        pending.append((slot, k))
        if len(pending) > 1:
            pass_on()

    for copy in local:
        copy.wait()
    for k in range(PIECES):
        score(OWN, k)
    for k in range(PIECES):
        behind(k)
        relay(k)
        score(PAIR, k)
        score(AHEAD, k)
    for k in range(PIECES):
        score(BEHIND, k)
        score(RELAY, k)
    pass_on()

    offsets = (0, step, -step, pair - r, r - pair)
    targets = [lax.rem(r + offset + nrows, nrows) for offset in offsets]
    nblk, nslots = lists_ref.shape[0], lists_ref.shape[1] - 1
    present = []
    for slot in range(1, SLOTS):
        flags = []
        for c in range(nblk):
            flag = jnp.int32(0)
            for k in range(nslots):
                hit = jnp.logical_and(k < lists_ref[c, nslots], lists_ref[c, k] == targets[slot])
                flag = jnp.maximum(flag, jnp.where(hit, jnp.int32(1), jnp.int32(0)))
            flags.append(flag)
        present.append(flags)

    for key in first:
        first[key][1].wait_recv()
        second[key].wait_recv()

    tile = 32
    keys = [(slot, k) for slot in range(SLOTS) for k in range(PIECES)]

    def flags_of(slot, which):
        flags = present[slot - 1]
        on = jnp.full((tile, unit), flags[0], jnp.int32)
        for c in range(1, nblk):
            on = jnp.where(which == c, flags[c], on)
        return on

    @pl.loop(0, share // tile)
    def _(i):
        at = pl.ds(pl.multiple_of(i * tile, tile), tile)
        row = w * share + i * tile + lax.broadcasted_iota(jnp.int32, (tile, unit), 0)
        col = lax.broadcasted_iota(jnp.int32, (tile, unit), 1)
        pos = lax.rem(row, block)
        which = row // block
        masks = [flags_of(slot, which) > 0 for slot in range(1, SLOTS)]
        left = col < small
        mixed = jnp.where(
            left, flags_of(BEHIND, which), flags_of(RELAY, which)) > 0
        masks[BEHIND - 1] = masks[RELAY - 1] = mixed
        logits, positives = [], []
        for slot, k in keys:
            s = (spart[slot, k, w, at] + rs1[slot, k, 0, at] + rs2r[slot, k, at]) * SCALE
            if slot == OWN:
                positives.append(jnp.where(col + k * unit == pos, s, 0.0))
            else:
                s = jnp.where(masks[slot - 1], s, -jnp.inf)
            logits.append(s)
        top = jnp.max(functools.reduce(jnp.maximum, logits), axis=1, keepdims=True)
        expon = [jnp.exp(s - top) for s in logits]
        total = jnp.sum(functools.reduce(jnp.add, expon), axis=1, keepdims=True)
        positive = jnp.sum(functools.reduce(jnp.add, positives), axis=1, keepdims=True)
        loss = top + jnp.log(total) - positive
        lossbuf[at] = jnp.broadcast_to(loss, (tile, lossbuf.shape[1]))
        factor = SCALE / total
        grads = {key: e * factor for key, e in zip(keys, expon)}
        for k in range(PIECES):
            one, two = grads[BEHIND, k], grads[RELAY, k]
            grads[BEHIND, k] = jnp.concatenate([one[:, :small], two[:, :small]], axis=1)
            grads[RELAY, k] = jnp.concatenate([one[:, small:], two[:, small:]], axis=1)
        for slot, k in keys:
            g = grads[slot, k]
            if slot == OWN:
                g = g - jnp.where(col + k * unit == pos, SCALE, 0.0)
            gbuf[slot, k, w, at] = g.astype(jnp.bfloat16)

    from_across, from_side, from_diagonal = {}, {}, {}
    for slot, k in RETURN_ORDER:
        mine = gbuf.at[slot, k, w]
        from_across[slot, k] = send(mine, mine, to_across)
        from_side[slot, k] = send(mine, mine, to_side)

    n = lossbuf.shape[1]
    eye = (lax.broadcasted_iota(jnp.int32, (share, n), 0)
           == lax.broadcasted_iota(jnp.int32, (share, n), 1))
    loss_ref[...] = jnp.sum(jnp.where(eye, lossbuf[...], 0.0), axis=0, keepdims=True)[:, :share]

    merged = {}
    tiles = 2
    cols = width // tiles

    def relay_grads(slot, k):
        from_across[slot, k].wait_recv()
        other = gbuf.at[slot, k, across]
        from_diagonal[slot, k] = send(other, other, to_side)

    def term_piece(slot, k):
        from_side[slot, k].wait_recv()
        from_diagonal[slot, k].wait_recv()
        grads = gbuf[slot, k].reshape(4 * share, unit)
        for j in range(tiles):
            at = slice(j * cols, (j + 1) * cols)
            term = dot(grads, q_ref[:, at], TN)
            if slot == OWN:
                term_own[piece[k], at] = term
            elif slot == AHEAD:
                term_ahead[piece[k], at] = term
            else:
                tsend[slot - 1, piece[k], at] = term.astype(jnp.bfloat16)
        if slot not in (OWN, AHEAD):
            device = to_behind if slot == BEHIND else to_pair
            merged[slot, k] = send(
                tsend.at[slot - 1, piece[k]], trecv.at[slot - 1, piece[k]], device)

    relay_grads(*RETURN_ORDER[0])
    for here, later in zip(RETURN_ORDER, RETURN_ORDER[1:] + (None,)):
        term_piece(*here)
        if later is not None:
            relay_grads(*later)
    for k in range(PIECES):
        merged[RELAY, k].wait_recv()
        both = term_ahead[piece[k]] + trecv[RELAY - 1, piece[k]].astype(jnp.float32)
        tsend[AHEAD - 1, piece[k]] = both.astype(jnp.bfloat16)
        merged[AHEAD, k] = send(
            tsend.at[AHEAD - 1, piece[k]], trecv.at[AHEAD - 1, piece[k]], to_ahead)

    tile_cols = 256

    @pl.loop(0, width // tile_cols)
    def _(j):
        at = pl.ds(pl.multiple_of(j * tile_cols, tile_cols), tile_cols)
        total = None
        for slot in range(SLOTS):
            for k in range(PIECES):
                rows = p_ref[piece[k], at] if slot == OWN else pbuf[slot - 1, piece[k], at]
                part = dot(gbuf[slot, k].reshape(4 * share, unit), rows, NN)
                total = part if total is None else total + part
        gq_ref[:, at] = total.astype(jnp.bfloat16)

    for k in range(PIECES):
        total = term_own[piece[k]]
        for slot in (PAIR, BEHIND, AHEAD):
            merged[slot, k].wait_recv()
            total += trecv[slot - 1, piece[k]].astype(jnp.float32)
        gp_ref[piece[k]] = total.astype(jnp.bfloat16)

    for copy in started:
        if id(copy) not in sent:
            copy.wait_send()


def store_kernel(*refs):
    *pairs, sems = refs
    half = len(pairs) // 2
    copies = [
        pltpu.make_async_copy(src, dst, sems.at[n])
        for n, (src, dst) in enumerate(zip(pairs[:half], pairs[half:]))
    ]
    for copy in copies:
        copy.start()
    for copy in copies:
        copy.wait()


def store(*arrays):
    return pl.pallas_call(
        store_kernel,
        out_shape=tuple(jax.ShapeDtypeStruct(a.shape, a.dtype) for a in arrays),
        in_specs=[pl.BlockSpec(memory_space=pl.ANY)] * len(arrays),
        out_specs=tuple(pl.BlockSpec(memory_space=pltpu.HBM) for a in arrays),
        scratch_shapes=[pltpu.SemaphoreType.DMA((len(arrays),))],
        compiler_params=pltpu.CompilerParams(vmem_limit_bytes=2 * 1024 * 1024),
    )(*arrays)


def per_device(queries, passages, neighbor_ids, counts):
    nrows = lax.axis_size("rows")
    assert lax.axis_size("width") == 4 and nrows % 2 == 0
    per_dev, width = queries.shape
    block = passages.shape[0]
    share = per_dev // 4
    unit = block // PIECES
    lanes = -(-share // 128) * 128
    vmem = pl.BlockSpec(memory_space=pltpu.VMEM)
    hbm = pl.BlockSpec(memory_space=pltpu.HBM)
    bf16, f32 = jnp.bfloat16, jnp.float32
    ncopies = copies_needed()
    lists = jnp.concatenate([neighbor_ids, counts[:, None]], axis=1)
    results = pl.pallas_call(
        functools.partial(kernel, nrows),
        out_shape=(
            jax.ShapeDtypeStruct((1, share), f32),
            jax.ShapeDtypeStruct((per_dev, width), bf16),
            jax.ShapeDtypeStruct((block, width), bf16),
        ),
        in_specs=[hbm, hbm, hbm],
        out_specs=(vmem, vmem, vmem),
        scratch_shapes=[
            pltpu.VMEM((SLOTS - 1, block, width), bf16),
            pltpu.VMEM((SLOTS, PIECES, 4, share, unit), f32),
            pltpu.VMEM((SLOTS, PIECES, 2, share, unit), f32),
            pltpu.VMEM((SLOTS, PIECES, share, unit), f32),
            pltpu.VMEM((SLOTS, PIECES, share, unit), f32),
            pltpu.VMEM((SLOTS, PIECES, 4, share, unit), bf16),
            pltpu.VMEM((share, lanes), f32),
            pltpu.VMEM((block, width), f32),
            pltpu.VMEM((block, width), f32),
            pltpu.VMEM((SLOTS - 1, block, width), bf16),
            pltpu.VMEM((SLOTS - 1, block, width), bf16),
            pltpu.SMEM(lists.shape, jnp.int32),
            pltpu.VMEM((per_dev, width), bf16),
            pltpu.VMEM((block, width), bf16),
            pltpu.SemaphoreType.DMA((3,)),
            pltpu.SemaphoreType.DMA((ncopies,)),
            pltpu.SemaphoreType.DMA((ncopies,)),
        ],
        compiler_params=pltpu.CompilerParams(
            collective_id=0, has_side_effects=True, vmem_limit_bytes=50 * 1024 * 1024
        ),
    )(lists, queries, passages)
    losses, grad_q, grad_p = store(*results)
    return losses.reshape(share), grad_q, grad_p


def solution(mesh):
    return jax.shard_map(
        per_device,
        mesh=mesh,
        in_specs=(P("rows", "width"), P("rows", "width"), P("rows", None), P("rows")),
        out_specs=(P(("rows", "width")), P("rows", "width"), P("rows", "width")),
        check_vma=False,
    )
```

```python
import functools

import jax
import jax.numpy as jnp
from jax import lax
from jax.experimental import pallas as pl
from jax.experimental.pallas import tpu as pltpu
from jax.sharding import PartitionSpec as P

MESH = pl.DeviceIdType.MESH
SCALE = 50.0
PIECES = 2
OWN, AHEAD, BEHIND, PAIR, RELAY = 0, 1, 2, 3, 4
SLOTS = 5
RETURN_ORDER = (
    (RELAY, 0), (BEHIND, 0), (RELAY, 1), (BEHIND, 1), (AHEAD, 0), (PAIR, 0), (AHEAD, 1), (PAIR, 1),
    (OWN, 0), (OWN, 1),
)

NT = (((1,), (1,)), ((), ()))
TN = (((0,), (0,)), ((), ()))
NN = (((1,), (0,)), ((), ()))


def dot(a, b, dims):
    return lax.dot_general(a, b, dims, preferred_element_type=jnp.float32)


def copies_needed():
    gather = 6 * PIECES
    scores = SLOTS * PIECES * 3
    grads = SLOTS * PIECES * 3
    terms = 4 * PIECES
    return gather + scores + grads + terms


def kernel(
    nrows, lists_hbm, q_hbm, p_hbm, loss_ref, gq_ref, gp_ref,
    pbuf, spart, rs1, rs2s, rs2r, gbuf, lossbuf, term_own, term_ahead,
    tsend, trecv, lists_ref, q_ref, p_ref, local_sem, send_sem, recv_sem,
):
    r = lax.axis_index("rows")
    w = lax.axis_index("width")
    par = lax.rem(r, 2)
    step = 2 - 4 * par
    pair = r + 1 - 2 * par
    ahead = lax.rem(r + step + nrows, nrows)
    behind = lax.rem(r - step + nrows, nrows)
    core = lax.rem(w, 2)
    side = w + 1 - 2 * core
    across = lax.rem(w + 2, 4)
    diagonal = lax.rem(side + 2, 4)
    block, width = p_ref.shape
    share = q_ref.shape[0] // 4

    to_pair, to_ahead, to_behind = {"rows": pair}, {"rows": ahead}, {"rows": behind}
    to_side, to_across = {"width": side}, {"width": across}

    local = [
        pltpu.make_async_copy(src, dst, local_sem.at[n])
        for n, (src, dst) in enumerate((
            (p_hbm, p_ref), (q_hbm, q_ref), (lists_hbm, lists_ref)))
    ]
    for copy in local:
        copy.start()

    barrier = pltpu.get_barrier_semaphore()
    for device in (to_pair, to_ahead, to_behind, to_side, to_across):
        pl.semaphore_signal(barrier, inc=1, device_id=device, device_id_type=MESH)
    pl.semaphore_wait(barrier, 5)

    started = []

    def send(src, dst, device):
        n = len(started)
        copy = pltpu.make_async_remote_copy(
            src_ref=src, dst_ref=dst, send_sem=send_sem.at[n], recv_sem=recv_sem.at[n],
            device_id=device, device_id_type=MESH,
        )
        copy.start()
        started.append(copy)
        return copy

    unit = block // PIECES
    piece = [pl.ds(k * unit, unit) for k in range(PIECES)]
    arrive = {}

    small = unit // 2
    strip = [pl.ds(m * small, small) for m in range(2 * PIECES)]

    def pass_block(slot, k, src, device):
        arrive[slot, k] = send(src.at[piece[k]], pbuf.at[slot - 1, piece[k]], device)

    def pass_strips(slot, k, src, device):
        for m in (2 * k, 2 * k + 1):
            arrive[slot, m] = send(src.at[strip[m]], pbuf.at[slot - 1, strip[m]], device)

    for k in range(PIECES):
        pass_block(AHEAD, k, p_hbm, to_behind)
        pass_block(PAIR, k, p_hbm, to_pair)
    sent = []

    def behind(k):
        arrive[AHEAD, k].wait_send()
        sent.append(id(arrive[AHEAD, k]))
        pass_strips(BEHIND, k, p_hbm, to_ahead)

    def relay(k):
        arrive[AHEAD, k].wait_recv()
        pass_strips(RELAY, k, pbuf.at[AHEAD - 1], to_pair)

    first, second, pending = {}, {}, []

    def pass_on():
        slot, k = pending.pop(0)
        first[slot, k][0].wait_recv()
        rs2s[slot, k] = spart[slot, k, across] + rs1[slot, k, 1]
        second[slot, k] = send(rs2s.at[slot, k], rs2r.at[slot, k], to_across)

    def score(slot, k):
        if slot in (BEHIND, RELAY):
            m = 2 * k + (slot == RELAY)
            arrive[BEHIND, m].wait_recv()
            arrive[RELAY, m].wait_recv()
            rows = jnp.concatenate(
                [pbuf[BEHIND - 1, strip[m]], pbuf[RELAY - 1, strip[m]]], axis=0)
        elif slot == OWN:
            rows = p_ref[piece[k]]
        else:
            if slot == PAIR:
                arrive[PAIR, k].wait_recv()
            rows = pbuf[slot - 1, piece[k]]
        spart[slot, k] = dot(q_ref[...], rows, NT).reshape(4, share, unit)
        first[slot, k] = (
            send(spart.at[slot, k, diagonal], rs1.at[slot, k, 1], to_side),
            send(spart.at[slot, k, side], rs1.at[slot, k, 0], to_side),
        )
        pending.append((slot, k))
        if len(pending) > 1:
            pass_on()

    for copy in local:
        copy.wait()
    for k in range(PIECES):
        score(OWN, k)
    for k in range(PIECES):
        behind(k)
        relay(k)
        score(PAIR, k)
        score(AHEAD, k)
    for k in range(PIECES):
        score(BEHIND, k)
        score(RELAY, k)
    pass_on()

    offsets = (0, step, -step, pair - r, r - pair)
    targets = [lax.rem(r + offset + nrows, nrows) for offset in offsets]
    nblk, nslots = lists_ref.shape[0], lists_ref.shape[1] - 1
    present = []
    for slot in range(1, SLOTS):
        flags = []
        for c in range(nblk):
            flag = jnp.int32(0)
            for k in range(nslots):
                hit = jnp.logical_and(k < lists_ref[c, nslots], lists_ref[c, k] == targets[slot])
                flag = jnp.maximum(flag, jnp.where(hit, jnp.int32(1), jnp.int32(0)))
            flags.append(flag)
        present.append(flags)

    for key in first:
        first[key][1].wait_recv()
        second[key].wait_recv()

    tile = 32
    keys = [(slot, k) for slot in range(SLOTS) for k in range(PIECES)]

    def flags_of(slot, which):
        flags = present[slot - 1]
        on = jnp.full((tile, unit), flags[0], jnp.int32)
        for c in range(1, nblk):
            on = jnp.where(which == c, flags[c], on)
        return on

    @pl.loop(0, share // tile, unroll=2)
    def _(i):
        at = pl.ds(pl.multiple_of(i * tile, tile), tile)
        row = w * share + i * tile + lax.broadcasted_iota(jnp.int32, (tile, unit), 0)
        col = lax.broadcasted_iota(jnp.int32, (tile, unit), 1)
        pos = lax.rem(row, block)
        which = row // block
        masks = [flags_of(slot, which) > 0 for slot in range(1, SLOTS)]
        left = col < small
        mixed = jnp.where(
            left, flags_of(BEHIND, which), flags_of(RELAY, which)) > 0
        masks[BEHIND - 1] = masks[RELAY - 1] = mixed
        logits, positives = [], []
        for slot, k in keys:
            s = (spart[slot, k, w, at] + rs1[slot, k, 0, at] + rs2r[slot, k, at]) * SCALE
            if slot == OWN:
                positives.append(jnp.where(col + k * unit == pos, s, 0.0))
            else:
                s = jnp.where(masks[slot - 1], s, -jnp.inf)
            logits.append(s)
        top = jnp.max(functools.reduce(jnp.maximum, logits), axis=1, keepdims=True)
        expon = [jnp.exp(s - top) for s in logits]
        total = jnp.sum(functools.reduce(jnp.add, expon), axis=1, keepdims=True)
        positive = jnp.sum(functools.reduce(jnp.add, positives), axis=1, keepdims=True)
        loss = top + jnp.log(total) - positive
        lossbuf[at] = jnp.broadcast_to(loss, (tile, lossbuf.shape[1]))
        factor = SCALE / total
        grads = {key: e * factor for key, e in zip(keys, expon)}
        for k in range(PIECES):
            one, two = grads[BEHIND, k], grads[RELAY, k]
            grads[BEHIND, k] = jnp.concatenate([one[:, :small], two[:, :small]], axis=1)
            grads[RELAY, k] = jnp.concatenate([one[:, small:], two[:, small:]], axis=1)
        for slot, k in keys:
            g = grads[slot, k]
            if slot == OWN:
                g = g - jnp.where(col + k * unit == pos, SCALE, 0.0)
            gbuf[slot, k, w, at] = g.astype(jnp.bfloat16)

    from_across, from_side, from_diagonal = {}, {}, {}
    for slot, k in RETURN_ORDER:
        mine = gbuf.at[slot, k, w]
        from_across[slot, k] = send(mine, mine, to_across)
        from_side[slot, k] = send(mine, mine, to_side)

    n = lossbuf.shape[1]
    eye = (lax.broadcasted_iota(jnp.int32, (share, n), 0)
           == lax.broadcasted_iota(jnp.int32, (share, n), 1))
    loss_ref[...] = jnp.sum(jnp.where(eye, lossbuf[...], 0.0), axis=0, keepdims=True)[:, :share]

    merged = {}
    tiles = 2
    cols = width // tiles

    def relay_grads(slot, k):
        from_across[slot, k].wait_recv()
        other = gbuf.at[slot, k, across]
        from_diagonal[slot, k] = send(other, other, to_side)

    def term_piece(slot, k):
        from_side[slot, k].wait_recv()
        from_diagonal[slot, k].wait_recv()
        grads = gbuf[slot, k].reshape(4 * share, unit)
        for j in range(tiles):
            at = slice(j * cols, (j + 1) * cols)
            term = dot(grads, q_ref[:, at], TN)
            if slot == OWN:
                term_own[piece[k], at] = term
            elif slot == AHEAD:
                term_ahead[piece[k], at] = term
            else:
                tsend[slot - 1, piece[k], at] = term.astype(jnp.bfloat16)
        if slot not in (OWN, AHEAD):
            device = to_behind if slot == BEHIND else to_pair
            merged[slot, k] = send(
                tsend.at[slot - 1, piece[k]], trecv.at[slot - 1, piece[k]], device)

    def merge(k):
        merged[RELAY, k].wait_recv()
        both = term_ahead[piece[k]] + trecv[RELAY - 1, piece[k]].astype(jnp.float32)
        tsend[AHEAD - 1, piece[k]] = both.astype(jnp.bfloat16)
        merged[AHEAD, k] = send(
            tsend.at[AHEAD - 1, piece[k]], trecv.at[AHEAD - 1, piece[k]], to_ahead)

    relay_grads(*RETURN_ORDER[0])
    for here, later in zip(RETURN_ORDER, RETURN_ORDER[1:] + (None,)):
        term_piece(*here)
        if later is not None:
            relay_grads(*later)
        if here == (PAIR, PIECES - 1):
            merge(0)
    for k in range(1, PIECES):
        merge(k)

    tile_cols = 256

    @pl.loop(0, width // tile_cols)
    def _(j):
        at = pl.ds(pl.multiple_of(j * tile_cols, tile_cols), tile_cols)
        total = None
        for slot in range(SLOTS):
            for k in range(PIECES):
                rows = p_ref[piece[k], at] if slot == OWN else pbuf[slot - 1, piece[k], at]
                part = dot(gbuf[slot, k].reshape(4 * share, unit), rows, NN)
                total = part if total is None else total + part
        gq_ref[:, at] = total.astype(jnp.bfloat16)

    for k in range(PIECES):
        total = term_own[piece[k]]
        for slot in (PAIR, BEHIND, AHEAD):
            merged[slot, k].wait_recv()
            total += trecv[slot - 1, piece[k]].astype(jnp.float32)
        gp_ref[piece[k]] = total.astype(jnp.bfloat16)

    for copy in started:
        if id(copy) not in sent:
            copy.wait_send()


def store_kernel(*refs):
    *pairs, sems = refs
    half = len(pairs) // 2
    copies = [
        pltpu.make_async_copy(src, dst, sems.at[n])
        for n, (src, dst) in enumerate(zip(pairs[:half], pairs[half:]))
    ]
    for copy in copies:
        copy.start()
    for copy in copies:
        copy.wait()


def store(*arrays):
    return pl.pallas_call(
        store_kernel,
        out_shape=tuple(jax.ShapeDtypeStruct(a.shape, a.dtype) for a in arrays),
        in_specs=[pl.BlockSpec(memory_space=pl.ANY)] * len(arrays),
        out_specs=tuple(pl.BlockSpec(memory_space=pltpu.HBM) for a in arrays),
        scratch_shapes=[pltpu.SemaphoreType.DMA((len(arrays),))],
        compiler_params=pltpu.CompilerParams(vmem_limit_bytes=2 * 1024 * 1024),
    )(*arrays)


def per_device(queries, passages, neighbor_ids, counts):
    nrows = lax.axis_size("rows")
    assert lax.axis_size("width") == 4 and nrows % 2 == 0
    per_dev, width = queries.shape
    block = passages.shape[0]
    share = per_dev // 4
    unit = block // PIECES
    lanes = -(-share // 128) * 128
    vmem = pl.BlockSpec(memory_space=pltpu.VMEM)
    hbm = pl.BlockSpec(memory_space=pltpu.HBM)
    bf16, f32 = jnp.bfloat16, jnp.float32
    ncopies = copies_needed()
    lists = jnp.concatenate([neighbor_ids, counts[:, None]], axis=1)
    results = pl.pallas_call(
        functools.partial(kernel, nrows),
        out_shape=(
            jax.ShapeDtypeStruct((1, share), f32),
            jax.ShapeDtypeStruct((per_dev, width), bf16),
            jax.ShapeDtypeStruct((block, width), bf16),
        ),
        in_specs=[hbm, hbm, hbm],
        out_specs=(vmem, vmem, vmem),
        scratch_shapes=[
            pltpu.VMEM((SLOTS - 1, block, width), bf16),
            pltpu.VMEM((SLOTS, PIECES, 4, share, unit), f32),
            pltpu.VMEM((SLOTS, PIECES, 2, share, unit), f32),
            pltpu.VMEM((SLOTS, PIECES, share, unit), f32),
            pltpu.VMEM((SLOTS, PIECES, share, unit), f32),
            pltpu.VMEM((SLOTS, PIECES, 4, share, unit), bf16),
            pltpu.VMEM((share, lanes), f32),
            pltpu.VMEM((block, width), f32),
            pltpu.VMEM((block, width), f32),
            pltpu.VMEM((SLOTS - 1, block, width), bf16),
            pltpu.VMEM((SLOTS - 1, block, width), bf16),
            pltpu.SMEM(lists.shape, jnp.int32),
            pltpu.VMEM((per_dev, width), bf16),
            pltpu.VMEM((block, width), bf16),
            pltpu.SemaphoreType.DMA((3,)),
            pltpu.SemaphoreType.DMA((ncopies,)),
            pltpu.SemaphoreType.DMA((ncopies,)),
        ],
        compiler_params=pltpu.CompilerParams(
            collective_id=0, has_side_effects=True, vmem_limit_bytes=50 * 1024 * 1024
        ),
    )(lists, queries, passages)
    losses, grad_q, grad_p = store(*results)
    return losses.reshape(share), grad_q, grad_p


def solution(mesh):
    return jax.shard_map(
        per_device,
        mesh=mesh,
        in_specs=(P("rows", "width"), P("rows", "width"), P("rows", None), P("rows")),
        out_specs=(P(("rows", "width")), P("rows", "width"), P("rows", "width")),
        check_vma=False,
    )
```
